32 devices in a mesh: island: 4 (over y, core), inner: 8 (over z, x).
Axes of the slice: x: 2, y: 2, z: 4, core: 2. Of those that a mesh axis runs over, the one named last changes fastest.
Arguments:
- particles: float32 [384, 128, 128], P(('island', 'inner')), may hold values from -6 to 6
- velocity_x: float32 [128, 128], replicated, may hold values from -1 to 1
- velocity_y: float32 [128, 128], replicated, may hold values from -1 to 1
- copy_lists: int32 [1, 1, 384], P(None, None, ('island', 'inner')), may hold values from 0 to 95, as said below
- migrants: int32 [1, 384], P(None, ('island', 'inner')), may hold values from 0 to 3
- noise: float32 [1, 1, 384, 4096], P(None, None, ('island', 'inner')), may hold values from -6 to 6
Outputs:
- final_states: float32 [384, 128, 128], P(('island', 'inner'))
The draws below stay inside these ranges and needn't reach their ends.
Inputs may be any that keep to these rules, and one draw needn't show every extreme that they name: copy_lists[c, r, k] counts particles within the slot's island. Group each island's particles into blocks of 12 in order (block j holds positions j * 12 to (j + 1) * 12 - 1); the 12 slots of one such block copy at most 2 distinct particles of any one block, and in every round some block of slots copies exactly 2 distinct particles of one block.
All inputs are finite; a program needn't handle non-finite values.
Results may differ from the reference program's by a relative error of at most 0.00002.
Values sent between devices are 32-bit elements; how exact they have to be, the bound alone decides.
A program may use at most 128 MiB of HBM per device.

```python
import jax
import jax.numpy as jnp

P_DEV = 12
G = 128
CAP = 2
STEPS = 6
ROUNDS = 1
CYCLES = 1
H = 64
P_ISL = 96
PARTICLES = 384
N_ISLAND = 4
N_INNER = 8


def draw_copy_lists(key, part):
    lead = CYCLES * ROUNDS * N_ISLAND
    key_weight, key_pick, key_base, key_offset = jax.random.split(jax.random.fold_in(key, 11), 4)
    exponent = jax.random.randint(key_weight, (lead, N_INNER), 0, 5)
    weights = jnp.left_shift(jnp.ones_like(exponent), exponent)
    cumulative = jnp.cumsum(weights, axis=-1)
    totals = cumulative[:, -1][:, None, None]
    uniform_ints = jax.random.randint(key_pick, (lead, N_INNER, P_DEV), 0, totals)
    source_dev = jnp.sum((cumulative[:, None, None, :] <= uniform_ints[..., None]).astype(jnp.int32), axis=-1)
    source_dev = source_dev.at[:, :, 1].set(source_dev[:, :, 0])
    base = jax.random.randint(key_base, (lead, N_INNER, N_INNER), 0, P_DEV)
    offset = jax.random.randint(key_offset, (lead, N_INNER, P_DEV), 0, CAP)
    offset = offset.at[:, :, 0].set(0).at[:, :, 1].set(CAP - 1)
    base_source = jnp.take_along_axis(base, source_dev, axis=2)
    local = (base_source + offset) % P_DEV
    value = source_dev * P_DEV + local
    return value.reshape(CYCLES, ROUNDS, N_ISLAND * N_INNER * P_DEV).astype(jnp.int32)


def plant(values, rng, low, high):
    longest = values.shape.index(max(values.shape))
    spots = []
    for shift in (0, 1):
        where = [jax.random.randint(jax.random.fold_in(rng, axis), (), 0, length) for axis, length in enumerate(values.shape)]
        where[longest] = (where[longest] + shift) % values.shape[longest]
        spots.append(tuple(where))
    return values.at[spots[0]].set(low).at[spots[1]].set(high)


def levels(rng, dims, cuts, smallest, largest):
    gain = 1.0
    for dim, shards_of in cuts:
        steps = jax.random.uniform(jax.random.fold_in(jax.random.fold_in(rng, 6), dim), (shards_of,), jnp.float32, smallest / len(cuts), largest / len(cuts))
        gain = gain * jnp.repeat(jnp.exp(steps), dims[dim] // shards_of).reshape((-1,) + (1,) * (len(dims) - 1 - dim))
    return gain


def scatter_about(stream_key, extent, deviation, bound, pieces=(), kind=jnp.bfloat16):
    array = deviation * jax.random.normal(stream_key, extent, jnp.float32)
    if pieces:
        array = array * levels(stream_key, extent, pieces, -0.22, 0.18)
    return jnp.clip(array, -bound, bound).astype(kind)


def setup_inputs(seed: int = 0) -> dict:
    streams_of = jax.random.split(jax.random.key(seed), 7)
    return {
        "particles": scatter_about(streams_of[0], (PARTICLES, G, G), 1.0, 6.0, ((0, 32),), jnp.float32),
        "velocity_x": jnp.clip(jax.random.uniform(streams_of[1], (G, G), jnp.float32, -1.0, 1.0), -1.0, 1.0),
        "velocity_y": jnp.clip(jax.random.uniform(streams_of[2], (G, G), jnp.float32, -1.0, 1.0), -1.0, 1.0),
        "copy_lists": draw_copy_lists(jax.random.fold_in(streams_of[6], 71), 0),
        "migrants": plant(jax.random.randint(streams_of[4], (CYCLES, PARTICLES), 0, N_ISLAND), jax.random.fold_in(streams_of[4], 1), 0, N_ISLAND - 1).astype(jnp.int32),
        "noise": scatter_about(streams_of[5], (CYCLES, ROUNDS, PARTICLES, H * H), 1.0, 6.0, ((2, 32),), jnp.float32),
    }


diffusion = 0.2
advection = 0.1
noise_gain = 0.3


def stencil(field, velocity_x, velocity_y):
    east = jnp.roll(field, -1, 1)
    west = jnp.roll(field, 1, 1)
    north = jnp.roll(field, -1, 2)
    south = jnp.roll(field, 1, 2)
    laplace = east + west + north + south - 4.0 * field
    transport = (velocity_x + field) * (east - west) + (velocity_y + field) * (north - south)
    return field + diffusion * laplace - advection * transport


def upsample(coarse):
    count = coarse.shape[0]
    half = G // 2
    shaped = coarse.reshape(count, half, 1, half, 1)
    return jnp.broadcast_to(shaped, (count, half, 2, half, 2)).reshape(count, G, G)


def reference(particles, velocity_x, velocity_y, copy_lists, migrants, noise):
    states = particles
    slots = jnp.arange(PARTICLES, dtype=jnp.int32)
    island_base = (slots // P_ISL) * P_ISL
    within = slots % P_ISL
    for cycle in range(CYCLES):
        for round_index in range(ROUNDS):
            states = states[(island_base + copy_lists[cycle, round_index]).astype(jnp.int32)]
            states = states + noise_gain * upsample(noise[cycle, round_index])
            for step in range(STEPS):
                states = stencil(states, velocity_x, velocity_y)
        states = states[(migrants[cycle] * P_ISL + within).astype(jnp.int32)]
    return states
```

```python
import functools

import jax
import jax.numpy as jnp
from jax import lax
from jax.experimental import pallas as pl
from jax.experimental.pallas import tpu as pltpu
from jax.sharding import PartitionSpec as P

CAP = 2
STEPS = 6
HALO = 8
CHUNKS = 4
GROUPS = 3
CORES = 2

diffusion = 0.2
advection = 0.1
noise_gain = 0.3

MESH = pl.DeviceIdType.MESH


def windows_of(grid):
    rows = grid // CHUNKS
    wins = [(HALO, 2 * rows - HALO, 1)]
    for c in range(2, CHUNKS):
        wins.append((wins[-1][1], (c + 1) * rows - HALO, c))
    wins[-1] = (wins[-1][0], grid + HALO, CHUNKS - 1)
    return wins


def pieces(first, last, size, grid):
    found = []
    row = first
    while row < last:
        wrapped = row % grid
        stop = min(last, row + size - wrapped % size)
        found.append((wrapped, wrapped + stop - row))
        row = stop
    return found


def join(parts):
    return parts[0] if len(parts) == 1 else jnp.concatenate(parts, axis=0)


def kernel(n_in, n_is, count, grid, *refs):
    lists, migr, part_hbm, vx_ref, vy_ref, noise_hbm, out_hbm = refs[:7]
    part, nz, up, req, send, vel, outv, pos = refs[7:15]
    rest = list(refs[15:])
    recv = rest[:CHUNKS]
    rest = rest[CHUNKS:]
    wins = windows_of(grid)
    n_win = len(wins)
    gath = [rest[w * GROUPS:(w + 1) * GROUPS] for w in range(n_win)]
    rest = rest[n_win * GROUPS:]
    (load_sem, req_send, req_recv, p_send, p_recv, y_send, y_recv,
     c_send, c_recv, f_send, f_recv, out_sem) = rest
    per = count // GROUPS
    rows = grid // CHUNKS
    n_y = n_is // CORES

    me = lax.axis_index("inner")
    isl = lax.axis_index("island")
    my_y = isl // CORES
    core = isl % CORES
    mate = my_y * CORES + (1 - core)

    def inner_of(o):
        return lax.rem(me + o, n_in)

    def y_of(o):
        return lax.rem(my_y + o, n_y) * CORES + core

    barrier = pltpu.get_barrier_semaphore()
    for o in range(1, n_in):
        pl.semaphore_signal(barrier, inc=1, device_id={"inner": inner_of(o)}, device_id_type=MESH)
    for o in range(1, n_y):
        pl.semaphore_signal(barrier, inc=1, device_id={"island": y_of(o)}, device_id_type=MESH)
    pl.semaphore_signal(barrier, inc=1, device_id={"island": mate}, device_id_type=MESH)

    load_part = pltpu.make_async_copy(part_hbm, part, load_sem.at[0])
    load_nz = pltpu.make_async_copy(noise_hbm, nz, load_sem.at[1])
    load_part.start()
    load_nz.start()

    lane = lax.broadcasted_iota(jnp.int32, (1, 128), 1)
    ids = [lists[0, q] for q in range(count)]
    row = jnp.full((1, 128), -1, jnp.int32)
    for q in range(count):
        row = jnp.where(lane == q, ids[q], row)
    req[me] = row

    pl.semaphore_wait(barrier, n_in - 1 + n_y - 1 + 1)

    def req_copy(o):
        return pltpu.make_async_remote_copy(
            src_ref=req.at[me], dst_ref=req.at[me],
            send_sem=req_send.at[o], recv_sem=req_recv.at[o],
            device_id={"inner": inner_of(o)}, device_id_type=MESH)

    def part_copy(c, o):
        return pltpu.make_async_remote_copy(
            src_ref=send.at[o - 1, :, pl.ds(c * rows, rows)],
            dst_ref=recv[c].at[pl.ds(CAP * me, CAP)],
            send_sem=p_send.at[c, o], recv_sem=p_recv.at[c, o],
            device_id={"inner": inner_of(o)}, device_id_type=MESH)

    for o in range(1, n_in):
        req_copy(o).start()

    def wanted(device):
        local = req[device] - me * count
        inside = (local >= 0) & (local < count)
        low = jnp.min(jnp.where(inside, local, count))
        high = jnp.max(jnp.where(inside, local, 0))
        return jnp.minimum(low, high), high

    for q in range(count):
        block = ids[q] // count
        later = jnp.int32(0)
        for other in range(count):
            if other != q:
                hit = (ids[other] >= block * count) & (ids[other] < ids[q])
                later = jnp.maximum(later, hit.astype(jnp.int32))
        pos[q] = block * CAP + later

    load_part.wait()
    low, high = wanted(me)
    for k, which in enumerate((low, high)):
        for c in range(CHUNKS):
            recv[c][CAP * me + k] = part[which, c * rows:(c + 1) * rows, :]

    for o in range(1, n_in):
        req_copy(n_in - o).wait_recv()
        low, high = wanted(inner_of(o))
        send[o - 1, 0] = part[low]
        send[o - 1, 1] = part[high]
        part_copy(0, o).start()
    for c in range(1, CHUNKS):
        for o in range(1, n_in):
            part_copy(c, o).start()

    vel[0] = advection * vx_ref[...]
    vel[1] = advection * vy_ref[...]
    load_nz.wait()
    from_lane = lax.broadcasted_iota(jnp.int32, (128, 128), 0)
    to_lane = lax.broadcasted_iota(jnp.int32, (128, 128), 1)
    spread = [(from_lane == half * 64 + to_lane // 2).astype(jnp.float32) for half in (0, 1)]
    packed = nz.shape[1]

    def upsample(q, carry):
        for half in (0, 1):
            wide = noise_gain * jnp.dot(
                nz[q], spread[half], precision=lax.Precision.HIGHEST,
                preferred_element_type=jnp.float32)
            for k in (0, 1):
                up[q, pl.ds(2 * half + k, packed, stride=4), :] = wide
        return carry

    lax.fori_loop(0, count, upsample, 0)

    def y_copy(w, g, o):
        mine = gath[w][g].at[pl.ds(isl * per, per)]
        return pltpu.make_async_remote_copy(
            src_ref=mine, dst_ref=mine,
            send_sem=y_send.at[w, g, o], recv_sem=y_recv.at[w, g, o],
            device_id={"island": y_of(o)}, device_id_type=MESH)

    def core_copy(w, g):
        mine = gath[w][g].at[pl.ds(isl * per, per)]
        return pltpu.make_async_remote_copy(
            src_ref=mine, dst_ref=mine,
            send_sem=c_send.at[w, g], recv_sem=c_recv.at[w, g],
            device_id={"island": mate}, device_id_type=MESH)

    def forward_copy(w, g, o):
        came = gath[w][g].at[pl.ds(y_of(n_y - o) * per, per)]
        return pltpu.make_async_remote_copy(
            src_ref=came, dst_ref=came,
            send_sem=f_send.at[w, g, o], recv_sem=f_recv.at[w, g, o],
            device_id={"island": mate}, device_id_type=MESH)

    def forward(w, g):
        for o in range(1, n_y):
            y_copy(w, g, o).wait_recv()
            forward_copy(w, g, o).start()

    def out_copies(w, g):
        first, last, _ = wins[w]
        made = []
        for k, (r0, r1) in enumerate(pieces(first, last, grid, grid)):
            made.append(pltpu.make_async_copy(
                outv.at[pl.ds(g * per, per), pl.ds(r0, r1 - r0)],
                out_hbm.at[pl.ds(g * per, per), pl.ds(r0, r1 - r0)],
                out_sem.at[w, g, k]))
        return made

    def pick(w, g):
        core_copy(w, g).wait_recv()
        for o in range(1, n_y):
            forward_copy(w, g, o).wait_recv()
        first, last, _ = wins[w]
        for i in range(per):
            q = g * per + i
            came = gath[w][g][migr[0, q] * per + i]
            at = 0
            for r0, r1 in pieces(first, last, grid, grid):
                outv[q, r0:r1, :] = came[at:at + r1 - r0]
                at += r1 - r0
        for copy in out_copies(w, g):
            copy.start()

    arrived = 0
    for w, (first, last, need) in enumerate(wins):
        while arrived <= need:
            for o in range(1, n_in):
                part_copy(arrived, o).wait_recv()
            arrived += 1
        ins = pieces(first - HALO, last + HALO, rows, grid)
        tall = last - first + 2 * HALO

        def slot(i, carry, g):
            q = g * per + i
            place = pos[q]
            u = join([recv[r0 // rows][place, r0 % rows:r0 % rows + r1 - r0, :] for r0, r1 in ins])
            u = u + join([up[q, r0:r1, :] for r0, r1 in ins])
            vx = join([vel[0, r0:r1, :] for r0, r1 in ins])
            vy = join([vel[1, r0:r1, :] for r0, r1 in ins])
            for _ in range(STEPS):
                east = pltpu.roll(u, tall - 1, 0)
                west = pltpu.roll(u, 1, 0)
                north = pltpu.roll(u, 127, 1)
                south = pltpu.roll(u, 1, 1)
                slow = advection * u
                flow = (vx + slow) * (east - west) + (vy + slow) * (north - south)
                u = (1.0 - 4.0 * diffusion) * u + diffusion * ((east + west) + (north + south)) - flow
            gath[w][g][isl * per + i] = u[HALO:tall - HALO]
            return carry

        for g in range(GROUPS):
            lax.fori_loop(0, per, functools.partial(slot, g=g), 0)
            for o in range(1, n_y):
                y_copy(w, g, o).start()
            core_copy(w, g).start()
        if w > 0:
            for g in range(GROUPS):
                forward(w - 1, g)
    for g in range(GROUPS):
        forward(n_win - 1, g)
    for w in range(n_win):
        for g in range(GROUPS):
            pick(w, g)

    for o in range(1, n_in):
        req_copy(o).wait_send()
        for c in range(CHUNKS):
            part_copy(c, o).wait_send()
    for w in range(n_win):
        for g in range(GROUPS):
            core_copy(w, g).wait_send()
            for o in range(1, n_y):
                y_copy(w, g, o).wait_send()
                forward_copy(w, g, o).wait_send()
            for copy in out_copies(w, g):
                copy.wait()


def body(particles, velocity_x, velocity_y, copy_lists, migrants, noise):
    n_in = lax.axis_size("inner")
    n_is = lax.axis_size("island")
    n_y = n_is // CORES
    count, grid, _ = particles.shape
    packed = noise.shape[-1] // 128
    rows = grid // CHUNKS
    per = count // GROUPS
    wins = windows_of(grid)
    dma = pltpu.SemaphoreType.DMA
    f32 = jnp.float32
    scratch = [
        pltpu.VMEM((count, grid, grid), f32),
        pltpu.VMEM((count, packed, 128), f32),
        pltpu.VMEM((count, grid, grid), f32),
        pltpu.VMEM((n_in, 1, 128), jnp.int32),
        pltpu.VMEM((n_in - 1, CAP, grid, grid), f32),
        pltpu.VMEM((2, grid, grid), f32),
        pltpu.VMEM((count, grid, grid), f32),
        pltpu.SMEM((count,), jnp.int32),
    ]
    scratch += [pltpu.VMEM((n_in * CAP, rows, grid), f32) for _ in range(CHUNKS)]
    for first, last, _ in wins:
        scratch += [pltpu.VMEM((n_is * per, last - first, grid), f32) for _ in range(GROUPS)]
    scratch += [
        dma((2,)),
        dma((n_in,)), dma((n_in,)),
        dma((CHUNKS, n_in)), dma((CHUNKS, n_in)),
        dma((len(wins), GROUPS, n_y)), dma((len(wins), GROUPS, n_y)),
        dma((len(wins), GROUPS)), dma((len(wins), GROUPS)),
        dma((len(wins), GROUPS, n_y)), dma((len(wins), GROUPS, n_y)),
        dma((len(wins), GROUPS, 2)),
    ]
    smem = pl.BlockSpec(memory_space=pltpu.SMEM)
    vmem = pl.BlockSpec(memory_space=pltpu.VMEM)
    anyw = pl.BlockSpec(memory_space=pl.ANY)
    return pl.pallas_call(
        functools.partial(kernel, n_in, n_is, count, grid),
        out_shape=jax.ShapeDtypeStruct(particles.shape, f32),
        in_specs=[smem, smem, anyw, vmem, vmem, anyw],
        out_specs=anyw,
        scratch_shapes=scratch,
        compiler_params=pltpu.CompilerParams(
            collective_id=0, has_side_effects=True, vmem_limit_bytes=48 * 1024 * 1024),
    )(copy_lists.reshape(1, count), migrants.reshape(1, count), particles,
      velocity_x, velocity_y, noise.reshape(count, packed, 128))


def solution(mesh):
    placed = (
        P(("island", "inner"), None, None),
        P(),
        P(),
        P(None, None, ("island", "inner")),
        P(None, ("island", "inner")),
        P(None, None, ("island", "inner"), None),
    )
    return jax.shard_map(
        body,
        mesh=mesh,
        in_specs=placed,
        out_specs=P(("island", "inner"), None, None),
        check_vma=False,
    )
```

```python
import functools

import jax
import jax.numpy as jnp
from jax import lax
from jax.experimental import pallas as pl
from jax.experimental.pallas import tpu as pltpu
from jax.sharding import PartitionSpec as P

CAP = 2
STEPS = 6
HALO = 8
CHUNKS = 4
GROUPS = 3
CORES = 2

diffusion = 0.2
advection = 0.1
noise_gain = 0.3

MESH = pl.DeviceIdType.MESH


def windows_of(grid):
    rows = grid // CHUNKS
    wins = [(HALO, 2 * rows - HALO, 1)]
    for c in range(2, CHUNKS):
        wins.append((wins[-1][1], (c + 1) * rows - HALO, c))
    wins[-1] = (wins[-1][0], grid + HALO, CHUNKS - 1)
    return wins


def pieces(first, last, size, grid):
    found = []
    row = first
    while row < last:
        wrapped = row % grid
        stop = min(last, row + size - wrapped % size)
        found.append((wrapped, wrapped + stop - row))
        row = stop
    return found


def join(parts):
    return parts[0] if len(parts) == 1 else jnp.concatenate(parts, axis=0)


def step(u, vx, vy):
    east = pltpu.roll(u, u.shape[0] - 1, 0)
    west = pltpu.roll(u, 1, 0)
    north = pltpu.roll(u, u.shape[1] - 1, 1)
    south = pltpu.roll(u, 1, 1)
    slow = advection * u
    flow = (vx + slow) * (east - west) + (vy + slow) * (north - south)
    return (1.0 - 4.0 * diffusion) * u + diffusion * ((east + west) + (north + south)) - flow


def kernel(n_in, n_is, count, grid, *refs):
    lists, migr, part_hbm, vx_ref, vy_ref, noise_hbm, out_hbm = refs[:7]
    part, nz, up, req, send, vel, outv, pos = refs[7:15]
    rest = list(refs[15:])
    recv = rest[:CHUNKS]
    rest = rest[CHUNKS:]
    wins = windows_of(grid)
    n_win = len(wins)
    gath = [rest[w * GROUPS:(w + 1) * GROUPS] for w in range(n_win)]
    rest = rest[n_win * GROUPS:]
    (load_sem, req_send, req_recv, p_send, p_recv, y_send, y_recv,
     c_send, c_recv, f_send, f_recv, out_sem) = rest
    per = count // GROUPS
    rows = grid // CHUNKS
    n_y = n_is // CORES

    me = lax.axis_index("inner")
    isl = lax.axis_index("island")
    my_y = isl // CORES
    core = isl % CORES
    mate = my_y * CORES + (1 - core)

    def inner_of(o):
        return lax.rem(me + o, n_in)

    def y_of(o):
        return lax.rem(my_y + o, n_y) * CORES + core

    barrier = pltpu.get_barrier_semaphore()
    for o in range(1, n_in):
        pl.semaphore_signal(barrier, inc=1, device_id={"inner": inner_of(o)}, device_id_type=MESH)
    for o in range(1, n_y):
        pl.semaphore_signal(barrier, inc=1, device_id={"island": y_of(o)}, device_id_type=MESH)
    pl.semaphore_signal(barrier, inc=1, device_id={"island": mate}, device_id_type=MESH)

    load_part = pltpu.make_async_copy(part_hbm, part, load_sem.at[0])
    loads = [
        pltpu.make_async_copy(noise_hbm, nz, load_sem.at[1]),
        pltpu.make_async_copy(vx_ref, vel.at[0], load_sem.at[2]),
        pltpu.make_async_copy(vy_ref, vel.at[1], load_sem.at[3]),
    ]
    load_part.start()
    for load in loads:
        load.start()

    lane = lax.broadcasted_iota(jnp.int32, (1, 128), 1)
    ids = [lists[0, q] for q in range(count)]
    row = jnp.full((1, 128), -1, jnp.int32)
    for q in range(count):
        row = jnp.where(lane == q, ids[q], row)
    req[me] = row

    pl.semaphore_wait(barrier, n_in - 1 + n_y - 1 + 1)

    def req_copy(o):
        return pltpu.make_async_remote_copy(
            src_ref=req.at[me], dst_ref=req.at[me],
            send_sem=req_send.at[o], recv_sem=req_recv.at[o],
            device_id={"inner": inner_of(o)}, device_id_type=MESH)

    def part_copy(c, o):
        return pltpu.make_async_remote_copy(
            src_ref=send.at[o - 1, :, pl.ds(c * rows, rows)],
            dst_ref=recv[c].at[pl.ds(CAP * me, CAP)],
            send_sem=p_send.at[c, o], recv_sem=p_recv.at[c, o],
            device_id={"inner": inner_of(o)}, device_id_type=MESH)

    for o in range(1, n_in):
        req_copy(o).start()

    def wanted(device):
        local = req[device] - me * count
        inside = (local >= 0) & (local < count)
        low = jnp.min(jnp.where(inside, local, count))
        high = jnp.max(jnp.where(inside, local, 0))
        return jnp.minimum(low, high), high

    for q in range(count):
        block = ids[q] // count
        later = jnp.int32(0)
        for other in range(count):
            if other != q:
                hit = (ids[other] >= block * count) & (ids[other] < ids[q])
                later = jnp.maximum(later, hit.astype(jnp.int32))
        pos[q] = block * CAP + later

    load_part.wait()
    low, high = wanted(me)
    for k, which in enumerate((low, high)):
        for c in range(CHUNKS):
            recv[c][CAP * me + k] = part[which, c * rows:(c + 1) * rows, :]

    for o in range(1, n_in):
        req_copy(n_in - o).wait_recv()
        low, high = wanted(inner_of(o))
        send[o - 1, 0] = part[low]
        send[o - 1, 1] = part[high]
        part_copy(0, o).start()
    for c in range(1, CHUNKS):
        for o in range(1, n_in):
            part_copy(c, o).start()

    for load in loads:
        load.wait()
    for k in (0, 1):
        vel[k] = advection * vel[k]
    from_lane = lax.broadcasted_iota(jnp.int32, (128, 128), 0)
    to_lane = lax.broadcasted_iota(jnp.int32, (128, 128), 1)
    spread = [(from_lane == half * 64 + to_lane // 2).astype(jnp.float32) for half in (0, 1)]
    packed = nz.shape[1]

    def upsample(q, carry):
        for half in (0, 1):
            wide = noise_gain * jnp.dot(
                nz[q], spread[half], precision=lax.Precision.HIGHEST,
                preferred_element_type=jnp.float32)
            for k in (0, 1):
                up[q, pl.ds(2 * half + k, packed, stride=4), :] = wide
        return carry

    lax.fori_loop(0, count, upsample, 0)

    def y_copy(w, g, o):
        mine = gath[w][g].at[pl.ds(isl * per, per)]
        return pltpu.make_async_remote_copy(
            src_ref=mine, dst_ref=mine,
            send_sem=y_send.at[w, g, o], recv_sem=y_recv.at[w, g, o],
            device_id={"island": y_of(o)}, device_id_type=MESH)

    def core_copy(w, g):
        mine = gath[w][g].at[pl.ds(isl * per, per)]
        return pltpu.make_async_remote_copy(
            src_ref=mine, dst_ref=mine,
            send_sem=c_send.at[w, g], recv_sem=c_recv.at[w, g],
            device_id={"island": mate}, device_id_type=MESH)

    def forward_copy(w, g, o):
        came = gath[w][g].at[pl.ds(y_of(n_y - o) * per, per)]
        return pltpu.make_async_remote_copy(
            src_ref=came, dst_ref=came,
            send_sem=f_send.at[w, g, o], recv_sem=f_recv.at[w, g, o],
            device_id={"island": mate}, device_id_type=MESH)

    def forward(w, g):
        for o in range(1, n_y):
            y_copy(w, g, o).wait_recv()
            forward_copy(w, g, o).start()

    def out_copies(w, g):
        first, last, _ = wins[w]
        made = []
        for k, (r0, r1) in enumerate(pieces(first, last, grid, grid)):
            made.append(pltpu.make_async_copy(
                outv.at[pl.ds(g * per, per), pl.ds(r0, r1 - r0)],
                out_hbm.at[pl.ds(g * per, per), pl.ds(r0, r1 - r0)],
                out_sem.at[w, g, k]))
        return made

    def pick(w, g):
        core_copy(w, g).wait_recv()
        for o in range(1, n_y):
            forward_copy(w, g, o).wait_recv()
        first, last, _ = wins[w]
        for i in range(per):
            q = g * per + i
            came = gath[w][g][migr[0, q] * per + i]
            at = 0
            for r0, r1 in pieces(first, last, grid, grid):
                outv[q, r0:r1, :] = came[at:at + r1 - r0]
                at += r1 - r0
        for copy in out_copies(w, g):
            copy.start()

    arrived = 0
    for w, (first, last, need) in enumerate(wins):
        while arrived <= need:
            for o in range(1, n_in):
                part_copy(arrived, o).wait_recv()
            arrived += 1
        ins = pieces(first - HALO, last + HALO, rows, grid)
        tall = last - first + 2 * HALO

        vx = join([vel[0, r0:r1, :] for r0, r1 in ins])
        vy = join([vel[1, r0:r1, :] for r0, r1 in ins])
        for g in range(GROUPS):
            fields = []
            for i in range(per):
                q = g * per + i
                place = pos[q]
                u = join([recv[r0 // rows][place, r0 % rows:r0 % rows + r1 - r0, :] for r0, r1 in ins])
                fields.append(u + join([up[q, r0:r1, :] for r0, r1 in ins]))
            for _ in range(STEPS):
                fields = [step(u, vx, vy) for u in fields]
            for i, u in enumerate(fields):
                gath[w][g][isl * per + i] = u[HALO:tall - HALO]
            for o in range(1, n_y):
                y_copy(w, g, o).start()
            core_copy(w, g).start()
        if w > 0:
            for g in range(GROUPS):
                forward(w - 1, g)
    for g in range(GROUPS):
        forward(n_win - 1, g)
    for w in range(n_win):
        for g in range(GROUPS):
            pick(w, g)

    for o in range(1, n_in):
        req_copy(o).wait_send()
        for c in range(CHUNKS):
            part_copy(c, o).wait_send()
    for w in range(n_win):
        for g in range(GROUPS):
            core_copy(w, g).wait_send()
            for o in range(1, n_y):
                y_copy(w, g, o).wait_send()
                forward_copy(w, g, o).wait_send()
            for copy in out_copies(w, g):
                copy.wait()


def body(particles, velocity_x, velocity_y, copy_lists, migrants, noise):
    n_in = lax.axis_size("inner")
    n_is = lax.axis_size("island")
    n_y = n_is // CORES
    count, grid, _ = particles.shape
    packed = noise.shape[-1] // 128
    rows = grid // CHUNKS
    per = count // GROUPS
    wins = windows_of(grid)
    dma = pltpu.SemaphoreType.DMA
    f32 = jnp.float32
    scratch = [
        pltpu.VMEM((count, grid, grid), f32),
        pltpu.VMEM((count, packed, 128), f32),
        pltpu.VMEM((count, grid, grid), f32),
        pltpu.VMEM((n_in, 1, 128), jnp.int32),
        pltpu.VMEM((n_in - 1, CAP, grid, grid), f32),
        pltpu.VMEM((2, grid, grid), f32),
        pltpu.VMEM((count, grid, grid), f32),
        pltpu.SMEM((count,), jnp.int32),
    ]
    scratch += [pltpu.VMEM((n_in * CAP, rows, grid), f32) for _ in range(CHUNKS)]
    for first, last, _ in wins:
        scratch += [pltpu.VMEM((n_is * per, last - first, grid), f32) for _ in range(GROUPS)]
    scratch += [
        dma((4,)),
        dma((n_in,)), dma((n_in,)),
        dma((CHUNKS, n_in)), dma((CHUNKS, n_in)),
        dma((len(wins), GROUPS, n_y)), dma((len(wins), GROUPS, n_y)),
        dma((len(wins), GROUPS)), dma((len(wins), GROUPS)),
        dma((len(wins), GROUPS, n_y)), dma((len(wins), GROUPS, n_y)),
        dma((len(wins), GROUPS, 2)),
    ]
    smem = pl.BlockSpec(memory_space=pltpu.SMEM)
    anyw = pl.BlockSpec(memory_space=pltpu.HBM)
    return pl.pallas_call(
        functools.partial(kernel, n_in, n_is, count, grid),
        out_shape=jax.ShapeDtypeStruct(particles.shape, f32),
        in_specs=[smem, smem, anyw, anyw, anyw, anyw],
        out_specs=anyw,
        scratch_shapes=scratch,
        compiler_params=pltpu.CompilerParams(
            collective_id=0, has_side_effects=True, vmem_limit_bytes=48 * 1024 * 1024),
    )(copy_lists.reshape(1, count), migrants.reshape(1, count), particles,
      velocity_x, velocity_y, noise.reshape(count, packed, 128))


def solution(mesh):
    placed = (
        P(("island", "inner"), None, None),
        P(),
        P(),
        P(None, None, ("island", "inner")),
        P(None, ("island", "inner")),
        P(None, None, ("island", "inner"), None),
    )
    return jax.shard_map(
        body,
        mesh=mesh,
        in_specs=placed,
        out_specs=P(("island", "inner"), None, None),
        check_vma=False,
    )
```

```python
import functools

import jax
import jax.numpy as jnp
from jax import lax
from jax.experimental import pallas as pl
from jax.experimental.pallas import tpu as pltpu
from jax.sharding import PartitionSpec as P

CAP = 2
STEPS = 6
HALO = 8
CHUNKS = 4
GROUPS = 3
CORES = 2

diffusion = 0.2
advection = 0.1
noise_gain = 0.3

MESH = pl.DeviceIdType.MESH


def windows_of(grid):
    rows = grid // CHUNKS
    wins = [(HALO, 2 * rows - HALO, 1)]
    for c in range(2, CHUNKS):
        wins.append((wins[-1][1], (c + 1) * rows - HALO, c))
    wins[-1] = (wins[-1][0], grid + HALO, CHUNKS - 1)
    return wins


def pieces(first, last, size, grid):
    found = []
    row = first
    while row < last:
        wrapped = row % grid
        stop = min(last, row + size - wrapped % size)
        found.append((wrapped, wrapped + stop - row))
        row = stop
    return found


def join(parts):
    return parts[0] if len(parts) == 1 else jnp.concatenate(parts, axis=0)


def step(u, vx, vy):
    east = pltpu.roll(u, u.shape[0] - 1, 0)
    west = pltpu.roll(u, 1, 0)
    north = pltpu.roll(u, u.shape[1] - 1, 1)
    south = pltpu.roll(u, 1, 1)
    slow = advection * u
    flow = (vx + slow) * (east - west) + (vy + slow) * (north - south)
    return (1.0 - 4.0 * diffusion) * u + diffusion * ((east + west) + (north + south)) - flow


def kernel(n_in, n_is, count, grid, *refs):
    lists, migr, part_hbm, vx_ref, vy_ref, noise_hbm, out_hbm = refs[:7]
    part, nz, up, req, send, vel, outv, pos = refs[7:15]
    rest = list(refs[15:])
    recv = rest[:CHUNKS]
    rest = rest[CHUNKS:]
    wins = windows_of(grid)
    n_win = len(wins)
    gath = [rest[w * GROUPS:(w + 1) * GROUPS] for w in range(n_win)]
    rest = rest[n_win * GROUPS:]
    (load_sem, req_send, req_recv, p_send, p_recv, y_send, y_recv,
     c_send, c_recv, f_send, f_recv, out_sem) = rest
    per = count // GROUPS
    rows = grid // CHUNKS
    n_y = n_is // CORES

    me = lax.axis_index("inner")
    isl = lax.axis_index("island")
    my_y = isl // CORES
    core = isl % CORES
    mate = my_y * CORES + (1 - core)

    def inner_of(o):
        return lax.rem(me + o, n_in)

    def y_of(o):
        return lax.rem(my_y + o, n_y) * CORES + core

    barrier = pltpu.get_barrier_semaphore()
    for o in range(1, n_in):
        pl.semaphore_signal(barrier, inc=1, device_id={"inner": inner_of(o)}, device_id_type=MESH)
    for o in range(1, n_y):
        pl.semaphore_signal(barrier, inc=1, device_id={"island": y_of(o)}, device_id_type=MESH)
    pl.semaphore_signal(barrier, inc=1, device_id={"island": mate}, device_id_type=MESH)

    load_part = pltpu.make_async_copy(part_hbm, part, load_sem.at[0])
    loads = [
        pltpu.make_async_copy(noise_hbm, nz, load_sem.at[1]),
        pltpu.make_async_copy(vx_ref, vel.at[0], load_sem.at[2]),
        pltpu.make_async_copy(vy_ref, vel.at[1], load_sem.at[3]),
    ]
    load_part.start()
    for load in loads:
        load.start()

    lane = lax.broadcasted_iota(jnp.int32, (1, 128), 1)
    ids = [lists[0, q] for q in range(count)]
    row = jnp.full((1, 128), -1, jnp.int32)
    for q in range(count):
        row = jnp.where(lane == q, ids[q], row)
    req[me] = row

    pl.semaphore_wait(barrier, n_in - 1 + n_y - 1 + 1)

    def req_copy(o):
        return pltpu.make_async_remote_copy(
            src_ref=req.at[me], dst_ref=req.at[me],
            send_sem=req_send.at[o], recv_sem=req_recv.at[o],
            device_id={"inner": inner_of(o)}, device_id_type=MESH)

    def part_copy(c, o):
        return pltpu.make_async_remote_copy(
            src_ref=send.at[o - 1, :, pl.ds(c * rows, rows)],
            dst_ref=recv[c].at[pl.ds(CAP * me, CAP)],
            send_sem=p_send.at[c, o], recv_sem=p_recv.at[c, o],
            device_id={"inner": inner_of(o)}, device_id_type=MESH)

    for o in range(1, n_in):
        req_copy(o).start()

    def wanted(device):
        local = req[device] - me * count
        inside = (local >= 0) & (local < count)
        low = jnp.min(jnp.where(inside, local, count))
        high = jnp.max(jnp.where(inside, local, 0))
        return jnp.minimum(low, high), high

    for q in range(count):
        block = ids[q] // count
        later = jnp.int32(0)
        for other in range(count):
            if other != q:
                hit = (ids[other] >= block * count) & (ids[other] < ids[q])
                later = jnp.maximum(later, hit.astype(jnp.int32))
        pos[q] = block * CAP + later

    load_part.wait()
    low, high = wanted(me)
    for k, which in enumerate((low, high)):
        for c in range(CHUNKS):
            recv[c][CAP * me + k] = part[which, c * rows:(c + 1) * rows, :]

    for o in range(1, n_in):
        req_copy(n_in - o).wait_recv()
        low, high = wanted(inner_of(o))
        send[o - 1, 0] = part[low]
        send[o - 1, 1] = part[high]
        part_copy(0, o).start()
    for c in range(1, CHUNKS):
        for o in range(1, n_in):
            part_copy(c, o).start()

    for load in loads:
        load.wait()
    for k in (0, 1):
        vel[k] = advection * vel[k]
    from_lane = lax.broadcasted_iota(jnp.int32, (128, 128), 0)
    to_lane = lax.broadcasted_iota(jnp.int32, (128, 128), 1)
    spread = [(from_lane == half * 64 + to_lane // 2).astype(jnp.float32) for half in (0, 1)]
    packed = nz.shape[1]

    def upsample(q, carry):
        for half in (0, 1):
            wide = noise_gain * jnp.dot(
                nz[q], spread[half], precision=lax.Precision.HIGHEST,
                preferred_element_type=jnp.float32)
            for k in (0, 1):
                up[q, pl.ds(2 * half + k, packed, stride=4), :] = wide
        return carry

    lax.fori_loop(0, count, upsample, 0)

    def y_copy(w, g, o):
        mine = gath[w][g].at[pl.ds(isl * per, per)]
        return pltpu.make_async_remote_copy(
            src_ref=mine, dst_ref=mine,
            send_sem=y_send.at[w, g, o], recv_sem=y_recv.at[w, g, o],
            device_id={"island": y_of(o)}, device_id_type=MESH)

    def core_copy(w, g):
        mine = gath[w][g].at[pl.ds(isl * per, per)]
        return pltpu.make_async_remote_copy(
            src_ref=mine, dst_ref=mine,
            send_sem=c_send.at[w, g], recv_sem=c_recv.at[w, g],
            device_id={"island": mate}, device_id_type=MESH)

    def forward_copy(w, g, o):
        came = gath[w][g].at[pl.ds(y_of(n_y - o) * per, per)]
        return pltpu.make_async_remote_copy(
            src_ref=came, dst_ref=came,
            send_sem=f_send.at[w, g, o], recv_sem=f_recv.at[w, g, o],
            device_id={"island": mate}, device_id_type=MESH)

    def forward(w, g):
        for o in range(1, n_y):
            y_copy(w, g, o).wait_recv()
            forward_copy(w, g, o).start()

    def out_copies(w, g):
        first, last, _ = wins[w]
        made = []
        for k, (r0, r1) in enumerate(pieces(first, last, grid, grid)):
            made.append(pltpu.make_async_copy(
                outv.at[pl.ds(g * per, per), pl.ds(r0, r1 - r0)],
                out_hbm.at[pl.ds(g * per, per), pl.ds(r0, r1 - r0)],
                out_sem.at[w, g, k]))
        return made

    def pick(w, g):
        core_copy(w, g).wait_recv()
        for o in range(1, n_y):
            forward_copy(w, g, o).wait_recv()
        first, last, _ = wins[w]
        for i in range(per):
            q = g * per + i
            came = gath[w][g][migr[0, q] * per + i]
            at = 0
            for r0, r1 in pieces(first, last, grid, grid):
                outv[q, r0:r1, :] = came[at:at + r1 - r0]
                at += r1 - r0
        for copy in out_copies(w, g):
            copy.start()

    arrived = 0
    for w, (first, last, need) in enumerate(wins):
        while arrived <= need:
            for o in range(1, n_in):
                part_copy(arrived, o).wait_recv()
            arrived += 1
        ins = pieces(first - HALO, last + HALO, rows, grid)
        tall = last - first + 2 * HALO

        vx = join([vel[0, r0:r1, :] for r0, r1 in ins])
        vy = join([vel[1, r0:r1, :] for r0, r1 in ins])
        for g in range(GROUPS):
            fields = []
            for i in range(per):
                q = g * per + i
                place = pos[q]
                u = join([recv[r0 // rows][place, r0 % rows:r0 % rows + r1 - r0, :] for r0, r1 in ins])
                fields.append(u + join([up[q, r0:r1, :] for r0, r1 in ins]))
            for _ in range(STEPS):
                fields = [step(u, vx, vy) for u in fields]
            for i, u in enumerate(fields):
                gath[w][g][isl * per + i] = u[HALO:tall - HALO]
            for o in range(1, n_y):
                y_copy(w, g, o).start()
            core_copy(w, g).start()
        if w > 0:
            for g in range(GROUPS):
                forward(w - 1, g)
    for g in range(GROUPS):
        forward(n_win - 1, g)
    for w in range(n_win):
        for g in range(GROUPS):
            pick(w, g)

    for o in range(1, n_in):
        req_copy(o).wait_send()
        for c in range(CHUNKS):
            part_copy(c, o).wait_send()
    for w in range(n_win):
        for g in range(GROUPS):
            core_copy(w, g).wait_send()
            for o in range(1, n_y):
                y_copy(w, g, o).wait_send()
                forward_copy(w, g, o).wait_send()
            for copy in out_copies(w, g):
                copy.wait()


def body(particles, velocity_x, velocity_y, copy_lists, migrants, noise):
    n_in = lax.axis_size("inner")
    n_is = lax.axis_size("island")
    n_y = n_is // CORES
    count, grid, _ = particles.shape
    packed = noise.shape[-1] // 128
    rows = grid // CHUNKS
    per = count // GROUPS
    wins = windows_of(grid)
    dma = pltpu.SemaphoreType.DMA
    f32 = jnp.float32
    scratch = [
        pltpu.VMEM((count, grid, grid), f32),
        pltpu.VMEM((count, packed, 128), f32),
        pltpu.VMEM((count, grid, grid), f32),
        pltpu.VMEM((n_in, 1, 128), jnp.int32),
        pltpu.VMEM((n_in - 1, CAP, grid, grid), f32),
        pltpu.VMEM((2, grid, grid), f32),
        pltpu.VMEM((count, grid, grid), f32),
        pltpu.SMEM((count,), jnp.int32),
    ]
    scratch += [pltpu.VMEM((n_in * CAP, rows, grid), f32) for _ in range(CHUNKS)]
    for first, last, _ in wins:
        scratch += [pltpu.VMEM((n_is * per, last - first, grid), f32) for _ in range(GROUPS)]
    scratch += [
        dma((4,)),
        dma((n_in,)), dma((n_in,)),
        dma((CHUNKS, n_in)), dma((CHUNKS, n_in)),
        dma((len(wins), GROUPS, n_y)), dma((len(wins), GROUPS, n_y)),
        dma((len(wins), GROUPS)), dma((len(wins), GROUPS)),
        dma((len(wins), GROUPS, n_y)), dma((len(wins), GROUPS, n_y)),
        dma((len(wins), GROUPS, 2)),
    ]
    smem = pl.BlockSpec(memory_space=pltpu.SMEM)
    anyw = pl.BlockSpec(memory_space=pltpu.HBM)
    return pl.pallas_call(
        functools.partial(kernel, n_in, n_is, count, grid),
        out_shape=jax.ShapeDtypeStruct(particles.shape, f32),
        in_specs=[smem, smem, anyw, anyw, anyw, anyw],
        out_specs=anyw,
        scratch_shapes=scratch,
        compiler_params=pltpu.CompilerParams(
            collective_id=0, has_side_effects=True, vmem_limit_bytes=67043328),
    )(copy_lists.reshape(1, count), migrants.reshape(1, count), particles,
      velocity_x, velocity_y, noise.reshape(count, packed, 128))


def solution(mesh):
    placed = (
        P(("island", "inner"), None, None),
        P(),
        P(),
        P(None, None, ("island", "inner")),
        P(None, ("island", "inner")),
        P(None, None, ("island", "inner"), None),
    )
    return jax.shard_map(
        body,
        mesh=mesh,
        in_specs=placed,
        out_specs=P(("island", "inner"), None, None),
        check_vma=False,
    )
```

```python
import functools

import jax
import jax.numpy as jnp
from jax import lax
from jax.experimental import pallas as pl
from jax.experimental.pallas import tpu as pltpu
from jax.sharding import PartitionSpec as P

CAP = 2
STEPS = 6
HALO = 8
CHUNKS = 4
GROUPS = 3
CORES = 2

diffusion = 0.2
advection = 0.1
noise_gain = 0.3

MESH = pl.DeviceIdType.MESH


def windows_of(grid):
    rows = grid // CHUNKS
    wins = [(HALO, 2 * rows - HALO, 1)]
    for c in range(2, CHUNKS):
        wins.append((wins[-1][1], (c + 1) * rows - HALO, c))
    wins[-1] = (wins[-1][0], grid + HALO, CHUNKS - 1)
    return wins


def pieces(first, last, size, grid):
    found = []
    row = first
    while row < last:
        wrapped = row % grid
        stop = min(last, row + size - wrapped % size)
        found.append((wrapped, wrapped + stop - row))
        row = stop
    return found


def join(parts):
    return parts[0] if len(parts) == 1 else jnp.concatenate(parts, axis=0)


def step(u, vx, vy):
    east = pltpu.roll(u, u.shape[0] - 1, 0)
    west = pltpu.roll(u, 1, 0)
    north = pltpu.roll(u, u.shape[1] - 1, 1)
    south = pltpu.roll(u, 1, 1)
    slow = advection * u
    flow = (vx + slow) * (east - west) + (vy + slow) * (north - south)
    return (1.0 - 4.0 * diffusion) * u + diffusion * ((east + west) + (north + south)) - flow


def kernel(n_in, n_is, count, grid, *refs):
    lists, migr, part_hbm, vx_ref, vy_ref, noise_hbm, out_hbm = refs[:7]
    part, nz, up, req, send, vel, outv, pos = refs[7:15]
    rest = list(refs[15:])
    recv = rest[:CHUNKS]
    rest = rest[CHUNKS:]
    wins = windows_of(grid)
    n_win = len(wins)
    gath = [rest[w * GROUPS:(w + 1) * GROUPS] for w in range(n_win)]
    rest = rest[n_win * GROUPS:]
    (load_sem, req_send, req_recv, p_send, p_recv, y_send, y_recv,
     c_send, c_recv, f_send, f_recv, out_sem) = rest
    per = count // GROUPS
    rows = grid // CHUNKS
    n_y = n_is // CORES

    me = lax.axis_index("inner")
    isl = lax.axis_index("island")
    my_y = isl // CORES
    core = isl % CORES
    mate = my_y * CORES + (1 - core)

    def inner_of(o):
        return lax.rem(me + o, n_in)

    def y_of(o):
        return lax.rem(my_y + o, n_y) * CORES + core

    barrier = pltpu.get_barrier_semaphore()
    for o in range(1, n_in):
        pl.semaphore_signal(barrier, inc=1, device_id={"inner": inner_of(o)}, device_id_type=MESH)
    for o in range(1, n_y):
        pl.semaphore_signal(barrier, inc=1, device_id={"island": y_of(o)}, device_id_type=MESH)
    pl.semaphore_signal(barrier, inc=1, device_id={"island": mate}, device_id_type=MESH)

    load_part = pltpu.make_async_copy(part_hbm, part, load_sem.at[0])
    loads = [
        pltpu.make_async_copy(noise_hbm, nz, load_sem.at[1]),
        pltpu.make_async_copy(vx_ref, vel.at[0], load_sem.at[2]),
        pltpu.make_async_copy(vy_ref, vel.at[1], load_sem.at[3]),
    ]
    load_part.start()
    for load in loads:
        load.start()

    lane = lax.broadcasted_iota(jnp.int32, (1, 128), 1)
    ids = [lists[0, q] for q in range(count)]
    row = jnp.full((1, 128), -1, jnp.int32)
    for q in range(count):
        row = jnp.where(lane == q, ids[q], row)
    req[me] = row

    pl.semaphore_wait(barrier, n_in - 1 + n_y - 1 + 1)

    def req_copy(o):
        return pltpu.make_async_remote_copy(
            src_ref=req.at[me], dst_ref=req.at[me],
            send_sem=req_send.at[o], recv_sem=req_recv.at[o],
            device_id={"inner": inner_of(o)}, device_id_type=MESH)

    def part_copy(c, o):
        return pltpu.make_async_remote_copy(
            src_ref=send.at[o - 1, :, pl.ds(c * rows, rows)],
            dst_ref=recv[c].at[pl.ds(CAP * me, CAP)],
            send_sem=p_send.at[c, o], recv_sem=p_recv.at[c, o],
            device_id={"inner": inner_of(o)}, device_id_type=MESH)

    for o in range(1, n_in):
        req_copy(o).start()

    def wanted(device):
        local = req[device] - me * count
        inside = (local >= 0) & (local < count)
        low = jnp.min(jnp.where(inside, local, count))
        high = jnp.max(jnp.where(inside, local, 0))
        return jnp.minimum(low, high), high

    for q in range(count):
        block = ids[q] // count
        later = jnp.int32(0)
        for other in range(count):
            if other != q:
                hit = (ids[other] >= block * count) & (ids[other] < ids[q])
                later = jnp.maximum(later, hit.astype(jnp.int32))
        pos[q] = block * CAP + later

    load_part.wait()
    low, high = wanted(me)
    for k, which in enumerate((low, high)):
        for c in range(CHUNKS):
            recv[c][CAP * me + k] = part[which, c * rows:(c + 1) * rows, :]

    for o in range(1, n_in):
        req_copy(n_in - o).wait_recv()
        low, high = wanted(inner_of(o))
        send[o - 1, 0] = part[low]
        send[o - 1, 1] = part[high]
        part_copy(0, o).start()
    for c in range(1, CHUNKS):
        for o in range(1, n_in):
            part_copy(c, o).start()

    for load in loads:
        load.wait()
    for k in (0, 1):
        vel[k] = advection * vel[k]
    from_lane = lax.broadcasted_iota(jnp.int32, (128, 128), 0)
    to_lane = lax.broadcasted_iota(jnp.int32, (128, 128), 1)
    spread = [(from_lane == half * 64 + to_lane // 2).astype(jnp.float32) for half in (0, 1)]
    packed = nz.shape[1]

    def upsample(q, carry):
        for half in (0, 1):
            wide = noise_gain * jnp.dot(
                nz[q], spread[half], precision=lax.Precision.HIGHEST,
                preferred_element_type=jnp.float32)
            for k in (0, 1):
                up[q, pl.ds(2 * half + k, packed, stride=4), :] = wide
        return carry

    lax.fori_loop(0, count, upsample, 0)

    def y_copy(w, g, o):
        mine = gath[w][g].at[pl.ds(isl * per, per)]
        return pltpu.make_async_remote_copy(
            src_ref=mine, dst_ref=mine,
            send_sem=y_send.at[w, g, o], recv_sem=y_recv.at[w, g, o],
            device_id={"island": y_of(o)}, device_id_type=MESH)

    def core_copy(w, g):
        mine = gath[w][g].at[pl.ds(isl * per, per)]
        return pltpu.make_async_remote_copy(
            src_ref=mine, dst_ref=mine,
            send_sem=c_send.at[w, g], recv_sem=c_recv.at[w, g],
            device_id={"island": mate}, device_id_type=MESH)

    def forward_copy(w, g, o):
        came = gath[w][g].at[pl.ds(y_of(n_y - o) * per, per)]
        return pltpu.make_async_remote_copy(
            src_ref=came, dst_ref=came,
            send_sem=f_send.at[w, g, o], recv_sem=f_recv.at[w, g, o],
            device_id={"island": mate}, device_id_type=MESH)

    def forward(w, g):
        for o in range(1, n_y):
            y_copy(w, g, o).wait_recv()
            forward_copy(w, g, o).start()

    def out_copies(w, g):
        first, last, _ = wins[w]
        made = []
        for k, (r0, r1) in enumerate(pieces(first, last, grid, grid)):
            made.append(pltpu.make_async_copy(
                outv.at[pl.ds(g * per, per), pl.ds(r0, r1 - r0)],
                out_hbm.at[pl.ds(g * per, per), pl.ds(r0, r1 - r0)],
                out_sem.at[w, g, k]))
        return made

    def pick(w, g):
        core_copy(w, g).wait_recv()
        for o in range(1, n_y):
            forward_copy(w, g, o).wait_recv()
        first, last, _ = wins[w]
        for i in range(per):
            q = g * per + i
            came = gath[w][g][migr[0, q] * per + i]
            at = 0
            for r0, r1 in pieces(first, last, grid, grid):
                outv[q, r0:r1, :] = came[at:at + r1 - r0]
                at += r1 - r0
        for copy in out_copies(w, g):
            copy.start()

    arrived = 0
    for w, (first, last, need) in enumerate(wins):
        while arrived <= need:
            for o in range(1, n_in):
                part_copy(arrived, o).wait_recv()
            arrived += 1
        ins = pieces(first - HALO, last + HALO, rows, grid)
        tall = last - first + 2 * HALO

        vx = join([vel[0, r0:r1, :] for r0, r1 in ins])
        vy = join([vel[1, r0:r1, :] for r0, r1 in ins])
        for g in range(GROUPS):
            fields = []
            for i in range(per):
                q = g * per + i
                place = pos[q]
                u = join([recv[r0 // rows][place, r0 % rows:r0 % rows + r1 - r0, :] for r0, r1 in ins])
                fields.append(u + join([up[q, r0:r1, :] for r0, r1 in ins]))
            for _ in range(STEPS):
                fields = [step(u, vx, vy) for u in fields]
            for i, u in enumerate(fields):
                gath[w][g][isl * per + i] = u[HALO:tall - HALO]
            for o in range(1, n_y):
                y_copy(w, g, o).start()
            core_copy(w, g).start()
        if w > 0:
            for g in range(GROUPS):
                forward(w - 1, g)
    for w in range(n_win - 1):
        for g in range(GROUPS):
            pick(w, g)
    for g in range(GROUPS):
        forward(n_win - 1, g)
    for g in range(GROUPS):
        pick(n_win - 1, g)

    for o in range(1, n_in):
        req_copy(o).wait_send()
        for c in range(CHUNKS):
            part_copy(c, o).wait_send()
    for w in range(n_win):
        for g in range(GROUPS):
            core_copy(w, g).wait_send()
            for o in range(1, n_y):
                y_copy(w, g, o).wait_send()
                forward_copy(w, g, o).wait_send()
            for copy in out_copies(w, g):
                copy.wait()


def body(particles, velocity_x, velocity_y, copy_lists, migrants, noise):
    n_in = lax.axis_size("inner")
    n_is = lax.axis_size("island")
    n_y = n_is // CORES
    count, grid, _ = particles.shape
    packed = noise.shape[-1] // 128
    rows = grid // CHUNKS
    per = count // GROUPS
    wins = windows_of(grid)
    dma = pltpu.SemaphoreType.DMA
    f32 = jnp.float32
    scratch = [
        pltpu.VMEM((count, grid, grid), f32),
        pltpu.VMEM((count, packed, 128), f32),
        pltpu.VMEM((count, grid, grid), f32),
        pltpu.VMEM((n_in, 1, 128), jnp.int32),
        pltpu.VMEM((n_in - 1, CAP, grid, grid), f32),
        pltpu.VMEM((2, grid, grid), f32),
        pltpu.VMEM((count, grid, grid), f32),
        pltpu.SMEM((count,), jnp.int32),
    ]
    scratch += [pltpu.VMEM((n_in * CAP, rows, grid), f32) for _ in range(CHUNKS)]
    for first, last, _ in wins:
        scratch += [pltpu.VMEM((n_is * per, last - first, grid), f32) for _ in range(GROUPS)]
    scratch += [
        dma((4,)),
        dma((n_in,)), dma((n_in,)),
        dma((CHUNKS, n_in)), dma((CHUNKS, n_in)),
        dma((len(wins), GROUPS, n_y)), dma((len(wins), GROUPS, n_y)),
        dma((len(wins), GROUPS)), dma((len(wins), GROUPS)),
        dma((len(wins), GROUPS, n_y)), dma((len(wins), GROUPS, n_y)),
        dma((len(wins), GROUPS, 2)),
    ]
    smem = pl.BlockSpec(memory_space=pltpu.SMEM)
    anyw = pl.BlockSpec(memory_space=pltpu.HBM)
    return pl.pallas_call(
        functools.partial(kernel, n_in, n_is, count, grid),
        out_shape=jax.ShapeDtypeStruct(particles.shape, f32),
        in_specs=[smem, smem, anyw, anyw, anyw, anyw],
        out_specs=anyw,
        scratch_shapes=scratch,
        compiler_params=pltpu.CompilerParams(
            collective_id=0, has_side_effects=True, vmem_limit_bytes=67043328),
    )(copy_lists.reshape(1, count), migrants.reshape(1, count), particles,
      velocity_x, velocity_y, noise.reshape(count, packed, 128))


def solution(mesh):
    placed = (
        P(("island", "inner"), None, None),
        P(),
        P(),
        P(None, None, ("island", "inner")),
        P(None, ("island", "inner")),
        P(None, None, ("island", "inner"), None),
    )
    return jax.shard_map(
        body,
        mesh=mesh,
        in_specs=placed,
        out_specs=P(("island", "inner"), None, None),
        check_vma=False,
    )
```
